32 devices in a mesh: seq: 8 (over z, x), head: 4 (over y, core).
Axes of the slice: x: 2, y: 2, z: 4, core: 2. Of those that a mesh axis runs over, the one named last changes fastest.
Arguments:
- queries: bfloat16 [4096, 4096], P('seq', 'head'), may hold values from -360 to 360, as said below
- key_rows: bfloat16 [4096, 1024], P('seq', 'head'), may hold values from -6 to 6
- value_rows: bfloat16 [4096, 1024], P('seq', 'head'), may hold values from -6 to 6
- doc_lengths: int32 [8], replicated, may hold values from 1 to 1536, 4096 in all
Outputs:
- attn_out: bfloat16 [4096, 4096], P(('seq', 'head'))
The draws below stay inside these ranges and needn't reach their ends.
Inputs may be any that keep to these rules, and one draw needn't show every extreme that they name: `queries`: custom draw of bounded query entries. `doc_lengths`: the lengths sum to 4096; each is at most 1536.
All inputs are finite; a program needn't handle non-finite values.
Results may differ from the reference program's by a relative error of at most 0.0036.
Values may be sent and summed in bfloat16 or wider, within the bound.
A program may use at most 64 MiB of HBM per device.

```python
import math
import jax
import jax.numpy as jnp
import numpy as np
from jax import lax

H = 32
KVH = 8
HD = 128
TOK_DEV = 512
SPAN = 4
TOKENS = 4096
MAXDOC = 1536
NDOCS = 8
N_SEQ = 8


def draw_queries(key, part):
    base = jnp.clip(jax.random.normal(key, (TOKENS, H * HD), jnp.float32), -4.5, 4.5)
    return base.astype(jnp.bfloat16)


def block_scale(own_key, shape, pieces, low, high):
    gain, own = 1.0, jax.random.fold_in(own_key, 6)
    for position, parts in pieces:
        heights = jnp.exp(jax.random.uniform(jax.random.fold_in(own, position), (parts,), jnp.float32, low / len(pieces), high / len(pieces)))
        gain = gain * jnp.repeat(heights, shape[position] // parts).reshape([-1 if axis == position else 1 for axis in range(len(shape))])
    return gain


def split_up(count, total, limit, slope):
    portions = [(1 << 20) // math.isqrt(standing ** slope) + 1 for standing in range(2, count + 1)]
    rest, counts = total - limit - (count - 1), [1] * (count - 1)
    while rest > 0:
        free = [i for i in range(count - 1) if counts[i] < limit]
        whole, left = sum([portions[i] for i in free]), rest
        for i in free:
            extra = min(limit - counts[i], max(1, left * portions[i] // whole), rest)
            counts[i] = counts[i] + extra
            rest = rest - extra
    return np.array([limit] + counts)


def ragged(key, amount, total, limit, slope):
    if amount == 2:
        one = jax.random.randint(key, (), max(1, total - limit), min(limit, total - 1) + 1)
        return jnp.stack([one, total - one])
    lengths = jnp.asarray(split_up(amount, total, limit, slope), jnp.int32)
    couples = (amount - 1) // 2
    source_of, sink = lengths[1:1 + 2 * couples:2], lengths[2:2 + 2 * couples:2]
    room = jnp.minimum(source_of - 1, limit - sink)
    passed = jax.random.randint(jax.random.fold_in(key, 1), (couples,), 0, 1 << 20) % (room + 1)
    lengths = lengths.at[1:1 + 2 * couples:2].set(source_of - passed).at[2:2 + 2 * couples:2].set(sink + passed)
    return lengths[jax.random.permutation(jax.random.fold_in(key, 2), amount)]


def noise(stream_key, shape, deviation, limit, split=(), kind=jnp.bfloat16):
    result = jax.random.normal(stream_key, shape, jnp.float32) * deviation
    if len(split) > 0:
        result = block_scale(stream_key, shape, split, -0.22, 0.18) * result
    return jnp.clip(result, min=-limit, max=limit).astype(kind)


def setup_inputs(seed: int = 0) -> dict:
    streams_of = jax.random.split(jax.random.key(seed), 5)
    return {
        "queries": draw_queries(jax.random.fold_in(streams_of[4], 71), 0),
        "key_rows": noise(streams_of[1], (TOKENS, KVH * HD), 1.0, 6.0, ((0, 8), (1, 4))),
        "value_rows": noise(streams_of[2], (TOKENS, KVH * HD), 1.0, 6.0, ((0, 8), (1, 4))),
        "doc_lengths": ragged(streams_of[3], NDOCS, TOKENS, MAXDOC, 2).astype(jnp.int32),
    }


scaling = 0.08838834764831845


def doc_index(ends, positions):
    return jnp.sum((ends[None, :] <= positions[:, None]).astype(jnp.int32), axis=1)


def reference(queries, key_rows, value_rows, doc_lengths):
    ends = jnp.cumsum(doc_lengths).astype(jnp.int32)
    group = H // KVH
    width = SPAN * TOK_DEV
    margin = (SPAN - 1) * TOK_DEV
    key_padded = jnp.concatenate([jnp.zeros((margin, KVH * HD), key_rows.dtype), key_rows], 0)
    value_padded = jnp.concatenate([jnp.zeros((margin, KVH * HD), value_rows.dtype), value_rows], 0)

    def block(index):
        start = (index * TOK_DEV).astype(jnp.int32)
        query_block = lax.dynamic_slice_in_dim(queries, start, TOK_DEV, 0).astype(jnp.float32).reshape(TOK_DEV, KVH, group, HD)
        key_block = lax.dynamic_slice_in_dim(key_padded, start, width, 0).astype(jnp.float32).reshape(width, KVH, HD)
        value_block = lax.dynamic_slice_in_dim(value_padded, start, width, 0).astype(jnp.float32).reshape(width, KVH, HD)
        query_pos = start + jnp.arange(TOK_DEV, dtype=jnp.int32)
        key_pos = start - margin + jnp.arange(width, dtype=jnp.int32)
        allowed = (key_pos[None, :] >= 0) & (doc_index(ends, key_pos)[None, :] == doc_index(ends, query_pos)[:, None]) & (key_pos[None, :] <= query_pos[:, None])
        scores = jnp.einsum("qgjd,kgd->gjqk", query_block, key_block, precision=lax.Precision.HIGHEST) * scaling
        scores = jnp.where(allowed[None, None], scores, jnp.float32(-1e30))
        largest = jnp.max(scores, axis=-1, keepdims=True)
        weights = jnp.where(allowed[None, None], jnp.exp(scores - largest), jnp.float32(0.0))
        total = jnp.sum(weights, axis=-1)
        rounded = lax.optimization_barrier(weights.astype(jnp.bfloat16)).astype(jnp.float32)
        output = jnp.einsum("gjqk,kgd->qgjd", rounded, value_block, precision=lax.Precision.HIGHEST)
        output = output / jnp.transpose(total, (2, 0, 1))[:, :, :, None]
        return output.reshape(TOK_DEV, H * HD).astype(jnp.bfloat16)

    blocks = lax.map(block, jnp.arange(N_SEQ, dtype=jnp.int32))
    return blocks.reshape(TOKENS, H * HD)
```

```python
import functools
import math

import jax
import jax.numpy as jnp
from jax import lax
from jax.experimental import pallas as pl
from jax.experimental.pallas import tpu as pltpu
from jax.sharding import PartitionSpec as P

H = 32
KVH = 8
HD = 128
SPAN = 4
FAR = -1e30
GROUP = H // KVH
EXP2_SCALE = 0.08838834764831845 * math.log2(math.e)
MESH = pl.DeviceIdType.MESH


def kernel(
    n_seq, n_head, doc_ref, q_hbm, k_hbm, v_hbm, out_ref,
    qbuf, kbuf, vbuf, qdoc, kdoc, obuf,
    load_sem, send_sem, recv_sem, out_send, out_recv, own_sem,
):
    b = lax.axis_index("seq")
    h = lax.axis_index("head")
    tokens = q_hbm.shape[0]
    groups = k_hbm.shape[1] // HD
    tile = tokens // n_head
    width = GROUP * HD
    window = SPAN * tokens
    reach = (SPAN - 1) * tokens
    even = b % 2 == 0
    odd = b % 2 == 1
    bufs = (kbuf, vbuf)

    loads = []
    for g in range(groups):
        for a, source in enumerate((k_hbm, v_hbm)):
            loads.append(pltpu.make_async_copy(
                source.at[:, pl.ds(g * HD, HD)],
                bufs[a].at[g, pl.ds(reach, tokens), :],
                load_sem.at[g, a],
            ))
    for load in loads:
        load.start()
    q_load = pltpu.make_async_copy(q_hbm, qbuf, load_sem.at[groups, 0])
    q_load.start()

    barrier = pltpu.get_barrier_semaphore()
    partner = b + 1 - 2 * (b % 2)
    pl.semaphore_signal(barrier, inc=1, device_id={"seq": partner, "head": h}, device_id_type=MESH)
    for off in range(1, n_head):
        pl.semaphore_signal(
            barrier, inc=1, device_id={"seq": b, "head": (h + off) % n_head}, device_id_type=MESH
        )

    @pl.when(b + 2 < n_seq)
    def _():
        pl.semaphore_signal(barrier, inc=1, device_id={"seq": b + 2, "head": h}, device_id_type=MESH)

    @pl.when(b >= 2)
    def _():
        pl.semaphore_signal(barrier, inc=1, device_id={"seq": b - 2, "head": h}, device_id_type=MESH)

    beyond = jnp.where(b + 2 < n_seq, 1, 0) + jnp.where(b >= 2, 1, 0)
    pl.semaphore_wait(barrier, n_head + beyond)

    def hop(kind, g, a, source, target, slot):
        return pltpu.make_async_remote_copy(
            src_ref=bufs[a].at[g, pl.ds(source * tokens, tokens), :],
            dst_ref=bufs[a].at[g, pl.ds(slot * tokens, tokens), :],
            send_sem=send_sem.at[kind, g, a],
            recv_sem=recv_sem.at[slot, g, a],
            device_id={"seq": target, "head": h},
            device_id_type=MESH,
        )

    own = SPAN - 1

    def send_own(g, a):
        @pl.when(even)
        def _():
            hop(0, g, a, own, b + 1, 2).start()

        @pl.when(b + 2 < n_seq)
        def _():
            hop(1, g, a, own, b + 2, 1).start()

    def relay_odd(g, a):
        @pl.when(odd & (b >= 2))
        def _():
            hop(1, g, a, own, b - 2, 1).wait_recv()
            hop(2, g, a, 1, b - 1, 2).start()

    def relay_even(g, a):
        @pl.when(even & (b >= 2))
        def _():
            hop(1, g, a, own, b - 2, 1).wait_recv()
            hop(2, g, a, 1, b + 1, 0).start()
            hop(2, g, a, own, b + 1, 2).wait_recv()

        @pl.when(even & (b >= 2) & (b + 2 < n_seq))
        def _():
            hop(3, g, a, 2, b + 2, 0).start()

    def arrive(g, a):
        @pl.when(odd)
        def _():
            hop(0, g, a, own, b - 1, 2).wait_recv()

        @pl.when(odd & (b >= 3))
        def _():
            hop(0, g, a, own, b - 1, 0).wait_recv()

        @pl.when(even & (b >= 4))
        def _():
            hop(0, g, a, own, b - 2, 0).wait_recv()

    def sent(g, a):
        @pl.when(even)
        def _():
            hop(0, g, a, own, b + 1, 2).wait_send()

        @pl.when(b + 2 < n_seq)
        def _():
            hop(1, g, a, own, b + 2, 1).wait_send()

        @pl.when(b >= 2)
        def _():
            hop(2, g, a, 1, partner, 0).wait_send()

        @pl.when(even & (b >= 2) & (b + 2 < n_seq))
        def _():
            hop(3, g, a, 2, b + 2, 0).wait_send()

    for a in range(2):
        loads[a].wait()
        send_own(0, a)
    for g in range(1, groups):
        for a in range(2):
            loads[g * 2 + a].wait()

            @pl.when(odd)
            def _():
                send_own(g, a)

    lane = lax.broadcasted_iota(jnp.int32, (1, HD), 1)
    low = jnp.full((1, HD), 1 << 30, jnp.int32)
    high = jnp.full((1, HD), 0, jnp.int32)
    end = jnp.int32(0)
    for d in range(doc_ref.shape[0]):
        start = end
        end = end + doc_ref[d]
        low = jnp.where(lane == d, start, low)
        high = jnp.where(lane == d, end, high)
    first = b * tokens

    def key_docs(i, _):
        rows = i * tile
        pos = first - reach + rows + lax.broadcasted_iota(jnp.int32, (tile, HD), 0)
        same = (pos >= low) & (pos < high)
        kdoc[pl.ds(rows, tile), :] = jnp.where(same, 0.0, FAR).astype(jnp.bfloat16)
        return 0

    lax.fori_loop(0, window // tile, key_docs, 0)

    def query_docs(i, _):
        rows = i * tile
        pos = first + rows + lax.broadcasted_iota(jnp.int32, (tile, HD), 0)
        same = (pos >= low) & (pos < high)
        qdoc[pl.ds(rows, tile), :] = jnp.where(same, 1.0, 0.0).astype(jnp.bfloat16)
        return 0

    lax.fori_loop(0, n_head, query_docs, 0)

    for slot in range(SPAN - 1):
        @pl.when(b < SPAN - 1 - slot)
        def _():
            for g in range(groups):
                for buf in bufs:
                    buf[g, slot * tokens:(slot + 1) * tokens, :] = jnp.zeros((tokens, HD), jnp.bfloat16)

    q_load.wait()
    for g in range(groups):
        for a in range(2):
            relay_odd(g, a)
    for a in range(2):
        relay_even(0, a)
    for g in range(1, groups):
        for a in range(2):
            @pl.when(even)
            def _():
                send_own(g, a)

    span = reach + tile
    ones = jnp.ones((span, HD), jnp.bfloat16)

    def deliver(g, off, t):
        return pltpu.make_async_remote_copy(
            src_ref=obuf.at[g, t],
            dst_ref=out_ref.at[:, pl.ds(pl.multiple_of((h * groups + g) * width, width), width)],
            send_sem=out_send.at[g, off - 1],
            recv_sem=out_recv.at[g, off - 1],
            device_id={"seq": b, "head": t},
            device_id_type=MESH,
        )

    def receive(g, off):
        source = (h + n_head - off) % n_head
        return pltpu.make_async_remote_copy(
            src_ref=obuf.at[g, 0],
            dst_ref=out_ref.at[:, pl.ds(pl.multiple_of((source * groups + g) * width, width), width)],
            send_sem=out_send.at[g, off - 1],
            recv_sem=out_recv.at[g, off - 1],
            device_id={"seq": b, "head": source},
            device_id_type=MESH,
        )

    def keep(g):
        return pltpu.make_async_copy(
            obuf.at[g, h],
            out_ref.at[:, pl.ds(pl.multiple_of((h * groups + g) * width, width), width)],
            own_sem.at[g],
        )

    def attend(g, t):
        rows = pl.ds(pl.multiple_of(t * tile, tile), tile)
        keys = pl.ds(pl.multiple_of(t * tile, tile), span)
        key_ext = jnp.concatenate([kbuf[g, keys, :], kdoc[keys, :]], 1)
        value_ext = jnp.concatenate([vbuf[g, keys, :], ones], 1)
        marks = qdoc[rows, :]
        below = lax.broadcasted_iota(jnp.int32, (tile, tile), 1) <= lax.broadcasted_iota(
            jnp.int32, (tile, tile), 0
        )
        pair = 2
        for part in range(GROUP // pair):
            query = jnp.concatenate([
                jnp.concatenate(
                    [qbuf[rows, (g * GROUP + part * pair + m) * HD:(g * GROUP + part * pair + m + 1) * HD], marks], 1
                )
                for m in range(pair)
            ], 0)
            scores = lax.dot_general(
                query, key_ext, (((1,), (1,)), ((), ())), preferred_element_type=jnp.float32
            )
            edge = jnp.where(jnp.concatenate([below] * pair, 0), scores[:, reach:], FAR)
            scores = jnp.concatenate([scores[:, :reach], edge], 1)
            largest = jnp.max(scores, axis=1, keepdims=True)
            weights = jnp.exp2((scores - largest) * EXP2_SCALE).astype(jnp.bfloat16)
            mixed = jnp.dot(weights, value_ext, preferred_element_type=jnp.float32)
            result = (mixed[:, :HD] / mixed[:, HD:]).astype(jnp.bfloat16)
            for m in range(pair):
                column = (part * pair + m) * HD
                obuf[g, t, :, column:column + HD] = result[m * tile:(m + 1) * tile]

    for g in range(groups):
        for a in range(2):
            arrive(g, a)

        def step(i, _):
            off = n_head - 1 - i
            t = (h + off) % n_head
            attend(g, t)
            if g + 1 < groups:
                @pl.when(i == 1)
                def _():
                    for a in range(2):
                        relay_even(g + 1, a)

            @pl.when(i < n_head - 1)
            def _():
                deliver(g, off, t).start()

            @pl.when(i == n_head - 1)
            def _():
                keep(g).start()
            return 0

        lax.fori_loop(0, n_head, step, 0)

    for g in range(groups):
        for a in range(2):
            sent(g, a)
    for g in range(groups):
        keep(g).wait()
        for off in range(1, n_head):
            deliver(g, off, (h + off) % n_head).wait_send()
            receive(g, off).wait_recv()


def per_device(n_seq, n_head, queries, key_rows, value_rows, doc_lengths):
    tokens = queries.shape[0]
    groups = key_rows.shape[1] // HD
    tile = tokens // n_head
    window = SPAN * tokens
    flops = 4 * tokens * (GROUP * groups) * window * HD
    return pl.pallas_call(
        functools.partial(kernel, n_seq, n_head),
        out_shape=jax.ShapeDtypeStruct((tile, H * HD), jnp.bfloat16),
        in_specs=[pl.BlockSpec(memory_space=pltpu.SMEM)]
        + [pl.BlockSpec(memory_space=pl.ANY)] * 3,
        out_specs=pl.BlockSpec(memory_space=pl.ANY),
        scratch_shapes=[
            pltpu.VMEM((tokens, GROUP * groups * HD), jnp.bfloat16),
            pltpu.VMEM((groups, window, HD), jnp.bfloat16),
            pltpu.VMEM((groups, window, HD), jnp.bfloat16),
            pltpu.VMEM((tokens, HD), jnp.bfloat16),
            pltpu.VMEM((window, HD), jnp.bfloat16),
            pltpu.VMEM((groups, n_head, tile, GROUP * HD), jnp.bfloat16),
            pltpu.SemaphoreType.DMA((groups + 1, 2)),
            pltpu.SemaphoreType.DMA((4, groups, 2)),
            pltpu.SemaphoreType.DMA((SPAN - 1, groups, 2)),
            pltpu.SemaphoreType.DMA((groups, n_head - 1)),
            pltpu.SemaphoreType.DMA((groups, n_head - 1)),
            pltpu.SemaphoreType.DMA((groups,)),
        ],
        compiler_params=pltpu.CompilerParams(
            collective_id=0, has_side_effects=True, vmem_limit_bytes=60 << 20
        ),
        cost_estimate=pl.CostEstimate(flops=flops, bytes_accessed=4 << 20, transcendentals=0),
    )(doc_lengths, queries, key_rows, value_rows)


def solution(mesh):
    body = functools.partial(per_device, mesh.shape["seq"], mesh.shape["head"])
    in_specs = (P("seq", "head"), P("seq", "head"), P("seq", "head"), P())
    out_specs = P(("seq", "head"), None)
    return jax.shard_map(body, mesh=mesh, in_specs=in_specs, out_specs=out_specs, check_vma=False)
```

```python
import functools
import math

import jax
import jax.numpy as jnp
from jax import lax
from jax.experimental import pallas as pl
from jax.experimental.pallas import tpu as pltpu
from jax.sharding import PartitionSpec as P

H = 32
KVH = 8
HD = 128
SPAN = 4
FAR = -1e30
PAIR = 2
GROUP = H // KVH
EXP2_SCALE = 0.08838834764831845 * math.log2(math.e)
MESH = pl.DeviceIdType.MESH


def kernel(
    n_seq, n_head, doc_ref, q_hbm, k_hbm, v_hbm, out_ref,
    qbuf, kbuf, vbuf, qdoc, kdoc, obuf, peak, total,
    load_sem, send_sem, recv_sem, out_send, out_recv, own_sem,
):
    b = lax.axis_index("seq")
    h = lax.axis_index("head")
    tokens = q_hbm.shape[0]
    groups = k_hbm.shape[1] // HD
    tile = tokens // n_head
    width = GROUP * HD
    window = SPAN * tokens
    reach = (SPAN - 1) * tokens
    even = b % 2 == 0
    odd = b % 2 == 1
    bufs = (kbuf, vbuf)

    loads = []
    for g in range(groups):
        for a, source in enumerate((k_hbm, v_hbm)):
            loads.append(pltpu.make_async_copy(
                source.at[:, pl.ds(g * HD, HD)],
                bufs[a].at[g, pl.ds(reach, tokens), :],
                load_sem.at[g, a],
            ))
    for load in loads:
        load.start()
    q_load = pltpu.make_async_copy(q_hbm, qbuf, load_sem.at[groups, 0])
    q_load.start()

    barrier = pltpu.get_barrier_semaphore()
    partner = b + 1 - 2 * (b % 2)
    outer = b - 1 + 2 * (b % 2)
    has_next = b + 2 < n_seq
    has_last = b >= 2
    has_outer = (outer >= 0) & (outer < n_seq)

    def greet(seq, head):
        pl.semaphore_signal(
            barrier, inc=1, device_id={"seq": seq, "head": head}, device_id_type=MESH
        )

    greet(partner, h)
    for off in range(1, n_head):
        greet(b, (h + off) % n_head)
    for condition, seq in ((has_next, b + 2), (has_last, b - 2), (has_outer, outer)):
        @pl.when(condition)
        def _():
            greet(seq, h)

    beyond = sum(jnp.where(c, 1, 0) for c in (has_next, has_last, has_outer))
    pl.semaphore_wait(barrier, n_head + beyond)

    own = SPAN - 1
    cut = tokens // 48 * 16

    def hop(kind, g, a, source, target, slot, piece=None):
        start, size = {None: (0, tokens), 0: (0, cut), 1: (cut, tokens - cut)}[piece]
        landing = slot if piece != 1 else own
        return pltpu.make_async_remote_copy(
            src_ref=bufs[a].at[g, pl.ds(source * tokens + start, size), :],
            dst_ref=bufs[a].at[g, pl.ds(slot * tokens + start, size), :],
            send_sem=send_sem.at[kind, g, a],
            recv_sem=recv_sem.at[landing, g, a],
            device_id={"seq": target, "head": h},
            device_id_type=MESH,
        )

    def own_near(g, a):
        return hop(0, g, a, own, b + 1, 2)

    def own_far(g, a):
        return hop(1, g, a, own, b + 2, 1)

    def even_one(g, a):
        return hop(2, g, a, 1, b + 1, 0, 1)

    def even_two(g, a):
        return hop(3, g, a, 2, b + 2, 0, 1)

    def odd_back(g, a):
        return hop(2, g, a, 1, b - 1, 2)

    def odd_one(g, a):
        return hop(3, g, a, 1, b + 1, 0, 0)

    def odd_two(g, a):
        return hop(4, g, a, 2, b + 2, 0, 0)

    sends = (
        (even, own_near),
        (has_next, own_far),
        (even & has_last, even_one),
        (even & has_last & has_next, even_two),
        (odd & has_last, odd_back),
        (odd & has_last & has_outer, odd_one),
        (odd & has_next, odd_two),
    )

    def send_own(g, a):
        for condition, copy in sends[:2]:
            @pl.when(condition)
            def _():
                copy(g, a).start()

    def relay_one(parity, g, a):
        if parity == 0:
            @pl.when(even & has_last)
            def _():
                hop(1, g, a, own, b - 2, 1).wait_recv()
                even_one(g, a).start()
        else:
            @pl.when(odd & has_last)
            def _():
                hop(1, g, a, own, b - 2, 1).wait_recv()
                odd_back(g, a).start()

            @pl.when(odd & has_last & has_outer)
            def _():
                odd_one(g, a).start()

    def relay_two(parity, g, a):
        if parity == 0:
            @pl.when(even & has_last)
            def _():
                hop(2, g, a, own, b + 1, 2).wait_recv()

            @pl.when(even & has_last & has_next)
            def _():
                even_two(g, a).start()
        else:
            @pl.when(odd)
            def _():
                hop(0, g, a, own, b - 1, 2).wait_recv()

            @pl.when(odd & has_next)
            def _():
                odd_two(g, a).start()

    def arrive(g, a):
        @pl.when(b >= SPAN - 1)
        def _():
            hop(2, g, a, 1, b - 1, 0, 0).wait_recv()
            hop(2, g, a, 1, b - 1, 0, 1).wait_recv()

    def sent(g, a):
        for condition, copy in sends:
            @pl.when(condition)
            def _():
                copy(g, a).wait_send()

    for g in range(groups):
        for a in range(2):
            loads[g * 2 + a].wait()
            send_own(g, a)

    lane = lax.broadcasted_iota(jnp.int32, (1, HD), 1)
    low = jnp.full((1, HD), 1 << 30, jnp.int32)
    high = jnp.full((1, HD), 0, jnp.int32)
    end = jnp.int32(0)
    for d in range(doc_ref.shape[0]):
        start = end
        end = end + doc_ref[d]
        low = jnp.where(lane == d, start, low)
        high = jnp.where(lane == d, end, high)
    first = b * tokens

    def key_docs(i, _):
        rows = i * tile
        pos = first - reach + rows + lax.broadcasted_iota(jnp.int32, (tile, HD), 0)
        same = (pos >= low) & (pos < high)
        kdoc[pl.ds(rows, tile), :] = jnp.where(same, 0.0, FAR).astype(jnp.bfloat16)
        return 0

    lax.fori_loop(0, window // tile, key_docs, 0)

    def query_docs(i, _):
        rows = i * tile
        pos = first + rows + lax.broadcasted_iota(jnp.int32, (tile, HD), 0)
        same = (pos >= low) & (pos < high)
        qdoc[pl.ds(rows, tile), :] = jnp.where(same, 1.0, 0.0).astype(jnp.bfloat16)
        return 0

    lax.fori_loop(0, n_head, query_docs, 0)

    for slot in range(SPAN - 1):
        @pl.when(b < SPAN - 1 - slot)
        def _():
            for g in range(groups):
                for buf in bufs:
                    buf[g, slot * tokens:(slot + 1) * tokens, :] = jnp.zeros((tokens, HD), jnp.bfloat16)

    q_load.wait()
    for a in range(2):
        relay_one(0, 0, a)
        relay_one(1, 0, a)
        relay_two(1, 0, a)
    for a in range(2):
        relay_two(0, 0, a)

    near = tokens * (SPAN - 2) + tile
    far = tokens

    def deliver(g, off, t):
        return pltpu.make_async_remote_copy(
            src_ref=obuf.at[g, t],
            dst_ref=out_ref.at[:, pl.ds(pl.multiple_of((h * groups + g) * width, width), width)],
            send_sem=out_send.at[g, off - 1],
            recv_sem=out_recv.at[g, off - 1],
            device_id={"seq": b, "head": t},
            device_id_type=MESH,
        )

    def receive(g, off):
        source = (h + n_head - off) % n_head
        return pltpu.make_async_remote_copy(
            src_ref=obuf.at[g, 0],
            dst_ref=out_ref.at[:, pl.ds(pl.multiple_of((source * groups + g) * width, width), width)],
            send_sem=out_send.at[g, off - 1],
            recv_sem=out_recv.at[g, off - 1],
            device_id={"seq": b, "head": source},
            device_id_type=MESH,
        )

    def keep(g):
        return pltpu.make_async_copy(
            obuf.at[g, h],
            out_ref.at[:, pl.ds(pl.multiple_of((h * groups + g) * width, width), width)],
            own_sem.at[g],
        )

    below = lax.broadcasted_iota(jnp.int32, (tile, tile), 1) <= lax.broadcasted_iota(
        jnp.int32, (tile, tile), 0
    )
    parts = GROUP // PAIR
    block = PAIR * tile

    def queries(g, t, part):
        rows = pl.ds(pl.multiple_of(t * tile, tile), tile)
        marks = qdoc[rows, :]
        return jnp.concatenate([
            jnp.concatenate([qbuf[rows, column:column + HD], marks], 1)
            for column in ((g * GROUP + part * PAIR + m) * HD for m in range(PAIR))
        ], 0)

    def window_of(g, start, size):
        keys = pl.ds(pl.multiple_of(start, tile), size)
        key_ext = jnp.concatenate([kbuf[g, keys, :], kdoc[keys, :]], 1)
        value_ext = jnp.concatenate([vbuf[g, keys, :], jnp.ones((size, HD), jnp.bfloat16)], 1)
        return key_ext, value_ext

    def attend_near(g, t):
        key_ext, value_ext = window_of(g, t * tile + far, near)
        for part in range(parts):
            scores = lax.dot_general(
                queries(g, t, part), key_ext, (((1,), (1,)), ((), ())),
                preferred_element_type=jnp.float32,
            )
            edge = jnp.where(jnp.concatenate([below] * PAIR, 0), scores[:, near - tile:], FAR)
            scores = jnp.concatenate([scores[:, :near - tile], edge], 1)
            largest = jnp.max(scores, axis=1, keepdims=True)
            weights = jnp.exp2((scores - largest) * EXP2_SCALE).astype(jnp.bfloat16)
            mixed = jnp.dot(weights, value_ext, preferred_element_type=jnp.float32)
            rows = slice(part * block, (part + 1) * block)
            peak[t, rows, :] = jnp.broadcast_to(largest, (block, HD))
            total[t, rows, :] = mixed

    def attend_far(g, t):
        key_ext, value_ext = window_of(g, t * tile, far)
        for part in range(parts):
            scores = lax.dot_general(
                queries(g, t, part), key_ext, (((1,), (1,)), ((), ())),
                preferred_element_type=jnp.float32,
            )
            rows = slice(part * block, (part + 1) * block)
            before = peak[t, rows, :]
            largest = jnp.maximum(jnp.max(scores, axis=1, keepdims=True), before)
            fade = jnp.exp2((before - largest) * EXP2_SCALE)
            weights = jnp.exp2(
                (scores - jnp.concatenate([largest] * (far // HD), 1)) * EXP2_SCALE
            ).astype(jnp.bfloat16)
            mixed = jnp.dot(weights, value_ext, preferred_element_type=jnp.float32)
            mixed = total[t, rows, :] * jnp.concatenate([fade, fade], 1) + mixed
            result = (mixed[:, :HD] / mixed[:, HD:]).astype(jnp.bfloat16)
            for m in range(PAIR):
                column = (part * PAIR + m) * HD
                obuf[g, t, :, column:column + HD] = result[m * tile:(m + 1) * tile]

    for g in range(groups):
        def near_step(i, _):
            attend_near(g, (h + n_head - 1 - i) % n_head)
            if g + 1 < groups:
                @pl.when(i == 0)
                def _():
                    relay_one(0, g + 1, 0)

                @pl.when(i == 1)
                def _():
                    relay_one(0, g + 1, 1)
                    relay_two(0, g + 1, 0)
                    relay_one(1, g + 1, 0)
                    relay_two(1, g + 1, 0)

                @pl.when(i == n_head - 1)
                def _():
                    relay_one(1, g + 1, 1)
                    relay_two(1, g + 1, 1)
                    relay_two(0, g + 1, 1)
            return 0

        lax.fori_loop(0, n_head, near_step, 0)
        for a in range(2):
            arrive(g, a)

        def far_step(i, _):
            off = n_head - 1 - i
            t = (h + off) % n_head
            attend_far(g, t)

            @pl.when(i < n_head - 1)
            def _():
                deliver(g, off, t).start()

            @pl.when(i == n_head - 1)
            def _():
                keep(g).start()
            return 0

        lax.fori_loop(0, n_head, far_step, 0)

    for g in range(groups):
        for a in range(2):
            sent(g, a)
    for g in range(groups):
        keep(g).wait()
        for off in range(1, n_head):
            deliver(g, off, (h + off) % n_head).wait_send()
            receive(g, off).wait_recv()


def per_device(n_seq, n_head, queries, key_rows, value_rows, doc_lengths):
    tokens = queries.shape[0]
    groups = key_rows.shape[1] // HD
    tile = tokens // n_head
    window = SPAN * tokens
    flops = 4 * tokens * (GROUP * groups) * window * HD
    return pl.pallas_call(
        functools.partial(kernel, n_seq, n_head),
        out_shape=jax.ShapeDtypeStruct((tile, H * HD), jnp.bfloat16),
        in_specs=[pl.BlockSpec(memory_space=pltpu.SMEM)]
        + [pl.BlockSpec(memory_space=pl.ANY)] * 3,
        out_specs=pl.BlockSpec(memory_space=pl.ANY),
        scratch_shapes=[
            pltpu.VMEM((tokens, GROUP * groups * HD), jnp.bfloat16),
            pltpu.VMEM((groups, window, HD), jnp.bfloat16),
            pltpu.VMEM((groups, window, HD), jnp.bfloat16),
            pltpu.VMEM((tokens, HD), jnp.bfloat16),
            pltpu.VMEM((window, HD), jnp.bfloat16),
            pltpu.VMEM((groups, n_head, tile, GROUP * HD), jnp.bfloat16),
            pltpu.VMEM((n_head, GROUP * tile, HD), jnp.float32),
            pltpu.VMEM((n_head, GROUP * tile, 2 * HD), jnp.float32),
            pltpu.SemaphoreType.DMA((groups + 1, 2)),
            pltpu.SemaphoreType.DMA((5, groups, 2)),
            pltpu.SemaphoreType.DMA((SPAN, groups, 2)),
            pltpu.SemaphoreType.DMA((groups, n_head - 1)),
            pltpu.SemaphoreType.DMA((groups, n_head - 1)),
            pltpu.SemaphoreType.DMA((groups,)),
        ],
        compiler_params=pltpu.CompilerParams(
            collective_id=0, has_side_effects=True, vmem_limit_bytes=60 << 20
        ),
        cost_estimate=pl.CostEstimate(flops=flops, bytes_accessed=4 << 20, transcendentals=0),
    )(doc_lengths, queries, key_rows, value_rows)


def solution(mesh):
    body = functools.partial(per_device, mesh.shape["seq"], mesh.shape["head"])
    in_specs = (P("seq", "head"), P("seq", "head"), P("seq", "head"), P())
    out_specs = P(("seq", "head"), None)
    return jax.shard_map(body, mesh=mesh, in_specs=in_specs, out_specs=out_specs, check_vma=False)
```

```python
import functools
import math

import jax
import jax.numpy as jnp
from jax import lax
from jax.experimental import pallas as pl
from jax.experimental.pallas import tpu as pltpu
from jax.sharding import PartitionSpec as P

H = 32
KVH = 8
HD = 128
SPAN = 4
FAR = -1e30
PAIR = 2
GROUP = H // KVH
EXP2_SCALE = 0.08838834764831845 * math.log2(math.e)
MESH = pl.DeviceIdType.MESH


def kernel(
    n_seq, n_head, doc_ref, q_hbm, k_hbm, v_hbm, out_ref,
    qbuf, kbuf, vbuf, qdoc, kdoc, obuf, peak, total,
    load_sem, send_sem, recv_sem, out_send, out_recv, own_sem,
):
    b = lax.axis_index("seq")
    h = lax.axis_index("head")
    tokens = q_hbm.shape[0]
    groups = k_hbm.shape[1] // HD
    tile = tokens // n_head
    width = GROUP * HD
    window = SPAN * tokens
    reach = (SPAN - 1) * tokens
    even = b % 2 == 0
    odd = b % 2 == 1
    bufs = (kbuf, vbuf)

    loads = []
    for g in range(groups):
        for a, source in enumerate((k_hbm, v_hbm)):
            loads.append(pltpu.make_async_copy(
                source.at[:, pl.ds(g * HD, HD)],
                bufs[a].at[g, pl.ds(reach, tokens), :],
                load_sem.at[g, a],
            ))
    for load in loads:
        load.start()
    q_load = pltpu.make_async_copy(q_hbm, qbuf, load_sem.at[groups, 0])
    q_load.start()

    barrier = pltpu.get_barrier_semaphore()
    partner = b + 1 - 2 * (b % 2)
    outer = b - 1 + 2 * (b % 2)
    has_next = b + 2 < n_seq
    has_last = b >= 2
    has_outer = (outer >= 0) & (outer < n_seq)

    def greet(seq, head):
        pl.semaphore_signal(
            barrier, inc=1, device_id={"seq": seq, "head": head}, device_id_type=MESH
        )

    greet(partner, h)
    for off in range(1, n_head):
        greet(b, (h + off) % n_head)
    for condition, seq in ((has_next, b + 2), (has_last, b - 2), (has_outer, outer)):
        @pl.when(condition)
        def _():
            greet(seq, h)

    beyond = sum(jnp.where(c, 1, 0) for c in (has_next, has_last, has_outer))
    pl.semaphore_wait(barrier, n_head + beyond)

    own = SPAN - 1
    cut = tokens // 48 * 16

    def hop(kind, g, a, source, target, slot, piece=None):
        start, size = {None: (0, tokens), 0: (0, cut), 1: (cut, tokens - cut)}[piece]
        landing = slot if piece != 1 else own
        return pltpu.make_async_remote_copy(
            src_ref=bufs[a].at[g, pl.ds(source * tokens + start, size), :],
            dst_ref=bufs[a].at[g, pl.ds(slot * tokens + start, size), :],
            send_sem=send_sem.at[kind, g, a],
            recv_sem=recv_sem.at[landing, g, a],
            device_id={"seq": target, "head": h},
            device_id_type=MESH,
        )

    def own_near(g, a):
        return hop(0, g, a, own, b + 1, 2)

    def own_far(g, a):
        return hop(1, g, a, own, b + 2, 1)

    def even_one(g, a):
        return hop(2, g, a, 1, b + 1, 0, 1)

    def even_two(g, a):
        return hop(3, g, a, 2, b + 2, 0, 1)

    def odd_back(g, a):
        return hop(2, g, a, 1, b - 1, 2)

    def odd_one(g, a):
        return hop(3, g, a, 1, b + 1, 0, 0)

    def odd_two(g, a):
        return hop(4, g, a, 2, b + 2, 0, 0)

    sends = (
        (even, own_near),
        (has_next, own_far),
        (even & has_last, even_one),
        (even & has_last & has_next, even_two),
        (odd & has_last, odd_back),
        (odd & has_last & has_outer, odd_one),
        (odd & has_next, odd_two),
    )

    def send_own(g, a):
        for condition, copy in sends[:2]:
            @pl.when(condition)
            def _():
                copy(g, a).start()

    def relay_one(parity, g, a):
        if parity == 0:
            @pl.when(even & has_last)
            def _():
                hop(1, g, a, own, b - 2, 1).wait_recv()
                even_one(g, a).start()
        else:
            @pl.when(odd & has_last)
            def _():
                hop(1, g, a, own, b - 2, 1).wait_recv()
                odd_back(g, a).start()

            @pl.when(odd & has_last & has_outer)
            def _():
                odd_one(g, a).start()

    def relay_two(parity, g, a):
        if parity == 0:
            @pl.when(even & has_last)
            def _():
                hop(2, g, a, own, b + 1, 2).wait_recv()

            @pl.when(even & has_last & has_next)
            def _():
                even_two(g, a).start()
        else:
            @pl.when(odd)
            def _():
                hop(0, g, a, own, b - 1, 2).wait_recv()

            @pl.when(odd & has_next)
            def _():
                odd_two(g, a).start()

    def arrive(g, a):
        @pl.when(b >= SPAN - 1)
        def _():
            hop(2, g, a, 1, b - 1, 0, 0).wait_recv()
            hop(2, g, a, 1, b - 1, 0, 1).wait_recv()

    def sent(g, a):
        for condition, copy in sends:
            @pl.when(condition)
            def _():
                copy(g, a).wait_send()

    for load in loads:
        load.wait()
    for a in range(2):
        send_own(0, a)
    for g in range(1, groups):
        send_own(g, 0)

    lane = lax.broadcasted_iota(jnp.int32, (1, HD), 1)
    low = jnp.full((1, HD), 1 << 30, jnp.int32)
    high = jnp.full((1, HD), 0, jnp.int32)
    end = jnp.int32(0)
    for d in range(doc_ref.shape[0]):
        start = end
        end = end + doc_ref[d]
        low = jnp.where(lane == d, start, low)
        high = jnp.where(lane == d, end, high)
    first = b * tokens

    def key_docs(i, _):
        rows = i * tile
        pos = first - reach + rows + lax.broadcasted_iota(jnp.int32, (tile, HD), 0)
        same = (pos >= low) & (pos < high)
        kdoc[pl.ds(rows, tile), :] = jnp.where(same, 0.0, FAR).astype(jnp.bfloat16)
        return 0

    lax.fori_loop(0, window // tile, key_docs, 0)

    def query_docs(i, _):
        rows = i * tile
        pos = first + rows + lax.broadcasted_iota(jnp.int32, (tile, HD), 0)
        same = (pos >= low) & (pos < high)
        qdoc[pl.ds(rows, tile), :] = jnp.where(same, 1.0, 0.0).astype(jnp.bfloat16)
        return 0

    lax.fori_loop(0, n_head, query_docs, 0)

    for slot in range(SPAN - 1):
        @pl.when(b < SPAN - 1 - slot)
        def _():
            for g in range(groups):
                for buf in bufs:
                    buf[g, slot * tokens:(slot + 1) * tokens, :] = jnp.zeros((tokens, HD), jnp.bfloat16)

    q_load.wait()
    for a in range(2):
        relay_one(0, 0, a)
        relay_one(1, 0, a)
        relay_two(1, 0, a)
    for a in range(2):
        relay_two(0, 0, a)
    for g in range(1, groups):
        send_own(g, 1)

    near = tokens * (SPAN - 2) + tile
    far = tokens

    def deliver(g, off, t):
        return pltpu.make_async_remote_copy(
            src_ref=obuf.at[g, t],
            dst_ref=out_ref.at[:, pl.ds(pl.multiple_of((h * groups + g) * width, width), width)],
            send_sem=out_send.at[g, off - 1],
            recv_sem=out_recv.at[g, off - 1],
            device_id={"seq": b, "head": t},
            device_id_type=MESH,
        )

    def receive(g, off):
        source = (h + n_head - off) % n_head
        return pltpu.make_async_remote_copy(
            src_ref=obuf.at[g, 0],
            dst_ref=out_ref.at[:, pl.ds(pl.multiple_of((source * groups + g) * width, width), width)],
            send_sem=out_send.at[g, off - 1],
            recv_sem=out_recv.at[g, off - 1],
            device_id={"seq": b, "head": source},
            device_id_type=MESH,
        )

    def keep(g):
        return pltpu.make_async_copy(
            obuf.at[g, h],
            out_ref.at[:, pl.ds(pl.multiple_of((h * groups + g) * width, width), width)],
            own_sem.at[g],
        )

    below = lax.broadcasted_iota(jnp.int32, (tile, tile), 1) <= lax.broadcasted_iota(
        jnp.int32, (tile, tile), 0
    )
    parts = GROUP // PAIR
    block = PAIR * tile

    def queries(g, t, part):
        rows = pl.ds(pl.multiple_of(t * tile, tile), tile)
        marks = qdoc[rows, :]
        return jnp.concatenate([
            jnp.concatenate([qbuf[rows, column:column + HD], marks], 1)
            for column in ((g * GROUP + part * PAIR + m) * HD for m in range(PAIR))
        ], 0)

    def window_of(g, start, size):
        keys = pl.ds(pl.multiple_of(start, tile), size)
        key_ext = jnp.concatenate([kbuf[g, keys, :], kdoc[keys, :]], 1)
        value_ext = jnp.concatenate([vbuf[g, keys, :], jnp.ones((size, HD), jnp.bfloat16)], 1)
        return key_ext, value_ext

    def attend_near(g, t):
        key_ext, value_ext = window_of(g, t * tile + far, near)
        every = [
            lax.dot_general(
                queries(g, t, part), key_ext, (((1,), (1,)), ((), ())),
                preferred_element_type=jnp.float32,
            )
            for part in range(parts)
        ]
        for part, scores in enumerate(every):
            edge = jnp.where(jnp.concatenate([below] * PAIR, 0), scores[:, near - tile:], FAR)
            scores = jnp.concatenate([scores[:, :near - tile], edge], 1)
            largest = jnp.max(scores, axis=1, keepdims=True)
            weights = jnp.exp2((scores - largest) * EXP2_SCALE).astype(jnp.bfloat16)
            mixed = jnp.dot(weights, value_ext, preferred_element_type=jnp.float32)
            rows = slice(part * block, (part + 1) * block)
            peak[t, rows, :] = jnp.broadcast_to(largest, (block, HD))
            total[t, rows, :] = mixed

    def attend_far(g, t):
        key_ext, value_ext = window_of(g, t * tile, far)
        every = [
            lax.dot_general(
                queries(g, t, part), key_ext, (((1,), (1,)), ((), ())),
                preferred_element_type=jnp.float32,
            )
            for part in range(parts)
        ]
        for part, scores in enumerate(every):
            rows = slice(part * block, (part + 1) * block)
            before = peak[t, rows, :]
            largest = jnp.maximum(jnp.max(scores, axis=1, keepdims=True), before)
            fade = jnp.exp2((before - largest) * EXP2_SCALE)
            weights = jnp.exp2(
                (scores - jnp.concatenate([largest] * (far // HD), 1)) * EXP2_SCALE
            ).astype(jnp.bfloat16)
            mixed = jnp.dot(weights, value_ext, preferred_element_type=jnp.float32)
            mixed = total[t, rows, :] * jnp.concatenate([fade, fade], 1) + mixed
            result = (mixed[:, :HD] / mixed[:, HD:]).astype(jnp.bfloat16)
            for m in range(PAIR):
                column = (part * PAIR + m) * HD
                obuf[g, t, :, column:column + HD] = result[m * tile:(m + 1) * tile]

    for g in range(groups):
        def near_step(i, _):
            attend_near(g, (h + n_head - 1 - i) % n_head)
            if g + 1 < groups:
                @pl.when(i == 1)
                def _():
                    relay_one(0, g + 1, 0)
                    relay_one(1, g + 1, 0)
                    relay_two(1, g + 1, 0)

                @pl.when(i == n_head - 1)
                def _():
                    relay_two(0, g + 1, 0)
            return 0

        lax.fori_loop(0, n_head, near_step, 0)
        for a in range(2):
            arrive(g, a)

        def far_step(i, _):
            off = n_head - 1 - i
            t = (h + off) % n_head
            attend_far(g, t)

            @pl.when(i < n_head - 1)
            def _():
                deliver(g, off, t).start()

            @pl.when(i == n_head - 1)
            def _():
                keep(g).start()

            if g + 1 < groups:
                @pl.when(i == n_head // 2)
                def _():
                    relay_one(0, g + 1, 1)
                    relay_one(1, g + 1, 1)
                    relay_two(1, g + 1, 1)

                @pl.when(i == n_head - 1)
                def _():
                    relay_two(0, g + 1, 1)
            return 0

        lax.fori_loop(0, n_head, far_step, 0)

    for g in range(groups):
        for a in range(2):
            sent(g, a)
    for g in range(groups):
        keep(g).wait()
        for off in range(1, n_head):
            deliver(g, off, (h + off) % n_head).wait_send()
            receive(g, off).wait_recv()


def per_device(n_seq, n_head, queries, key_rows, value_rows, doc_lengths):
    tokens = queries.shape[0]
    groups = key_rows.shape[1] // HD
    tile = tokens // n_head
    window = SPAN * tokens
    flops = 4 * tokens * (GROUP * groups) * window * HD
    return pl.pallas_call(
        functools.partial(kernel, n_seq, n_head),
        out_shape=jax.ShapeDtypeStruct((tile, H * HD), jnp.bfloat16),
        in_specs=[pl.BlockSpec(memory_space=pltpu.SMEM)]
        + [pl.BlockSpec(memory_space=pl.ANY)] * 3,
        out_specs=pl.BlockSpec(memory_space=pl.ANY),
        scratch_shapes=[
            pltpu.VMEM((tokens, GROUP * groups * HD), jnp.bfloat16),
            pltpu.VMEM((groups, window, HD), jnp.bfloat16),
            pltpu.VMEM((groups, window, HD), jnp.bfloat16),
            pltpu.VMEM((tokens, HD), jnp.bfloat16),
            pltpu.VMEM((window, HD), jnp.bfloat16),
            pltpu.VMEM((groups, n_head, tile, GROUP * HD), jnp.bfloat16),
            pltpu.VMEM((n_head, GROUP * tile, HD), jnp.float32),
            pltpu.VMEM((n_head, GROUP * tile, 2 * HD), jnp.float32),
            pltpu.SemaphoreType.DMA((groups + 1, 2)),
            pltpu.SemaphoreType.DMA((5, groups, 2)),
            pltpu.SemaphoreType.DMA((SPAN, groups, 2)),
            pltpu.SemaphoreType.DMA((groups, n_head - 1)),
            pltpu.SemaphoreType.DMA((groups, n_head - 1)),
            pltpu.SemaphoreType.DMA((groups,)),
        ],
        compiler_params=pltpu.CompilerParams(
            collective_id=0, has_side_effects=True, vmem_limit_bytes=60 << 20
        ),
        cost_estimate=pl.CostEstimate(flops=flops, bytes_accessed=4 << 20, transcendentals=0),
    )(doc_lengths, queries, key_rows, value_rows)


def solution(mesh):
    body = functools.partial(per_device, mesh.shape["seq"], mesh.shape["head"])
    in_specs = (P("seq", "head"), P("seq", "head"), P("seq", "head"), P())
    out_specs = P(("seq", "head"), None)
    return jax.shard_map(body, mesh=mesh, in_specs=in_specs, out_specs=out_specs, check_vma=False)
```

```python
import functools
import math

import jax
import jax.numpy as jnp
from jax import lax
from jax.experimental import pallas as pl
from jax.experimental.pallas import tpu as pltpu
from jax.sharding import PartitionSpec as P

H = 32
KVH = 8
HD = 128
SPAN = 4
FAR = -1e30
PAIR = 2
GROUP = H // KVH
EXP2_SCALE = 0.08838834764831845 * math.log2(math.e)
MESH = pl.DeviceIdType.MESH


def kernel(
    n_seq, n_head, doc_ref, q_hbm, k_hbm, v_hbm, out_ref,
    qbuf, kbuf, vbuf, qdoc, kdoc, obuf, peak, total,
    load_sem, send_sem, recv_sem, out_send, out_recv, own_sem,
):
    b = lax.axis_index("seq")
    h = lax.axis_index("head")
    tokens = q_hbm.shape[0]
    groups = k_hbm.shape[1] // HD
    tile = tokens // n_head
    width = GROUP * HD
    window = SPAN * tokens
    reach = (SPAN - 1) * tokens
    even = b % 2 == 0
    odd = b % 2 == 1
    bufs = (kbuf, vbuf)

    loads = []
    for g in range(groups):
        for a, source in enumerate((k_hbm, v_hbm)):
            loads.append(pltpu.make_async_copy(
                source.at[:, pl.ds(g * HD, HD)],
                bufs[a].at[g, pl.ds(reach, tokens), :],
                load_sem.at[g, a],
            ))
    for load in loads:
        load.start()
    q_load = pltpu.make_async_copy(q_hbm, qbuf, load_sem.at[groups, 0])
    q_load.start()

    barrier = pltpu.get_barrier_semaphore()
    partner = b + 1 - 2 * (b % 2)
    outer = b - 1 + 2 * (b % 2)
    has_next = b + 2 < n_seq
    has_last = b >= 2
    has_outer = (outer >= 0) & (outer < n_seq)

    def greet(seq, head):
        pl.semaphore_signal(
            barrier, inc=1, device_id={"seq": seq, "head": head}, device_id_type=MESH
        )

    greet(partner, h)
    for off in range(1, n_head):
        greet(b, (h + off) % n_head)
    for condition, seq in ((has_next, b + 2), (has_last, b - 2), (has_outer, outer)):
        @pl.when(condition)
        def _():
            greet(seq, h)

    beyond = sum(jnp.where(c, 1, 0) for c in (has_next, has_last, has_outer))
    pl.semaphore_wait(barrier, n_head + beyond)

    own = SPAN - 1
    cut = tokens // 64 * 16

    def hop(kind, g, a, source, target, slot, piece=None):
        start, size = {None: (0, tokens), 0: (0, cut), 1: (cut, tokens - cut)}[piece]
        landing = slot if piece != 1 else own
        return pltpu.make_async_remote_copy(
            src_ref=bufs[a].at[g, pl.ds(source * tokens + start, size), :],
            dst_ref=bufs[a].at[g, pl.ds(slot * tokens + start, size), :],
            send_sem=send_sem.at[kind, g, a],
            recv_sem=recv_sem.at[landing, g, a],
            device_id={"seq": target, "head": h},
            device_id_type=MESH,
        )

    def own_near(g, a):
        return hop(0, g, a, own, b + 1, 2)

    def own_far(g, a):
        return hop(1, g, a, own, b + 2, 1)

    def even_one(g, a):
        return hop(2, g, a, 1, b + 1, 0, 1)

    def even_two(g, a):
        return hop(3, g, a, 2, b + 2, 0, 1)

    def odd_back(g, a):
        return hop(2, g, a, 1, b - 1, 2)

    def odd_one(g, a):
        return hop(3, g, a, 1, b + 1, 0, 0)

    def odd_two(g, a):
        return hop(4, g, a, 2, b + 2, 0, 0)

    sends = (
        (even, own_near),
        (has_next, own_far),
        (even & has_last, even_one),
        (even & has_last & has_next, even_two),
        (odd & has_last, odd_back),
        (odd & has_last & has_outer, odd_one),
        (odd & has_next, odd_two),
    )

    def send_own(g, a):
        for condition, copy in sends[:2]:
            @pl.when(condition)
            def _():
                copy(g, a).start()

    def relay_one(parity, g, a):
        if parity == 0:
            @pl.when(even & has_last)
            def _():
                hop(1, g, a, own, b - 2, 1).wait_recv()
                even_one(g, a).start()
        else:
            @pl.when(odd & has_last)
            def _():
                hop(1, g, a, own, b - 2, 1).wait_recv()
                odd_back(g, a).start()

            @pl.when(odd & has_last & has_outer)
            def _():
                odd_one(g, a).start()

    def relay_two(parity, g, a):
        if parity == 0:
            @pl.when(even & has_last)
            def _():
                hop(2, g, a, own, b + 1, 2).wait_recv()

            @pl.when(even & has_last & has_next)
            def _():
                even_two(g, a).start()
        else:
            @pl.when(odd)
            def _():
                hop(0, g, a, own, b - 1, 2).wait_recv()

            @pl.when(odd & has_next)
            def _():
                odd_two(g, a).start()

    def arrive(g, a):
        @pl.when(b >= SPAN - 1)
        def _():
            hop(2, g, a, 1, b - 1, 0, 0).wait_recv()
            hop(2, g, a, 1, b - 1, 0, 1).wait_recv()

    def sent(g, a):
        for condition, copy in sends:
            @pl.when(condition)
            def _():
                copy(g, a).wait_send()

    for load in loads:
        load.wait()
    for a in range(2):
        send_own(0, a)
    for g in range(1, groups):
        send_own(g, 0)

    lane = lax.broadcasted_iota(jnp.int32, (1, HD), 1)
    low = jnp.full((1, HD), 1 << 30, jnp.int32)
    high = jnp.full((1, HD), 0, jnp.int32)
    end = jnp.int32(0)
    for d in range(doc_ref.shape[0]):
        start = end
        end = end + doc_ref[d]
        low = jnp.where(lane == d, start, low)
        high = jnp.where(lane == d, end, high)
    first = b * tokens

    def key_docs(i, _):
        rows = i * tile
        pos = first - reach + rows + lax.broadcasted_iota(jnp.int32, (tile, HD), 0)
        same = (pos >= low) & (pos < high)
        kdoc[pl.ds(rows, tile), :] = jnp.where(same, 0.0, FAR).astype(jnp.bfloat16)
        return 0

    lax.fori_loop(0, window // tile, key_docs, 0)

    def query_docs(i, _):
        rows = i * tile
        pos = first + rows + lax.broadcasted_iota(jnp.int32, (tile, HD), 0)
        same = (pos >= low) & (pos < high)
        qdoc[pl.ds(rows, tile), :] = jnp.where(same, 1.0, 0.0).astype(jnp.bfloat16)
        return 0

    lax.fori_loop(0, n_head, query_docs, 0)

    for slot in range(SPAN - 1):
        @pl.when(b < SPAN - 1 - slot)
        def _():
            for g in range(groups):
                for buf in bufs:
                    buf[g, slot * tokens:(slot + 1) * tokens, :] = jnp.zeros((tokens, HD), jnp.bfloat16)

    q_load.wait()
    for a in range(2):
        relay_one(0, 0, a)
        relay_one(1, 0, a)
        relay_two(1, 0, a)
    for a in range(2):
        relay_two(0, 0, a)
    for g in range(1, groups):
        send_own(g, 1)

    near = tokens * (SPAN - 2) + tile
    far = tokens

    def deliver(g, off, t):
        return pltpu.make_async_remote_copy(
            src_ref=obuf.at[g, t],
            dst_ref=out_ref.at[:, pl.ds(pl.multiple_of((h * groups + g) * width, width), width)],
            send_sem=out_send.at[g, off - 1],
            recv_sem=out_recv.at[g, off - 1],
            device_id={"seq": b, "head": t},
            device_id_type=MESH,
        )

    def receive(g, off):
        source = (h + n_head - off) % n_head
        return pltpu.make_async_remote_copy(
            src_ref=obuf.at[g, 0],
            dst_ref=out_ref.at[:, pl.ds(pl.multiple_of((source * groups + g) * width, width), width)],
            send_sem=out_send.at[g, off - 1],
            recv_sem=out_recv.at[g, off - 1],
            device_id={"seq": b, "head": source},
            device_id_type=MESH,
        )

    def keep(g):
        return pltpu.make_async_copy(
            obuf.at[g, h],
            out_ref.at[:, pl.ds(pl.multiple_of((h * groups + g) * width, width), width)],
            own_sem.at[g],
        )

    below = lax.broadcasted_iota(jnp.int32, (tile, tile), 1) <= lax.broadcasted_iota(
        jnp.int32, (tile, tile), 0
    )
    parts = GROUP // PAIR
    block = PAIR * tile

    def queries(g, t, part):
        rows = pl.ds(pl.multiple_of(t * tile, tile), tile)
        marks = qdoc[rows, :]
        return jnp.concatenate([
            jnp.concatenate([qbuf[rows, column:column + HD], marks], 1)
            for column in ((g * GROUP + part * PAIR + m) * HD for m in range(PAIR))
        ], 0)

    def window_of(g, start, size):
        keys = pl.ds(pl.multiple_of(start, tile), size)
        key_ext = jnp.concatenate([kbuf[g, keys, :], kdoc[keys, :]], 1)
        return key_ext, vbuf[g, keys, :]

    def mix(weights, values):
        mixed = jnp.dot(weights.astype(jnp.bfloat16), values, preferred_element_type=jnp.float32)
        amount = jnp.sum(weights, axis=1, keepdims=True)
        return jnp.concatenate([mixed, jnp.broadcast_to(amount, (block, HD))], 1)

    def attend_near(g, t):
        key_ext, value_ext = window_of(g, t * tile + far, near)
        every = [
            lax.dot_general(
                queries(g, t, part), key_ext, (((1,), (1,)), ((), ())),
                preferred_element_type=jnp.float32,
            )
            for part in range(parts)
        ]
        for part, scores in enumerate(every):
            edge = jnp.where(jnp.concatenate([below] * PAIR, 0), scores[:, near - tile:], FAR)
            scores = jnp.concatenate([scores[:, :near - tile], edge], 1)
            largest = jnp.max(scores, axis=1, keepdims=True)
            weights = jnp.exp2((scores - largest) * EXP2_SCALE)
            mixed = mix(weights, value_ext)
            rows = slice(part * block, (part + 1) * block)
            peak[t, rows, :] = jnp.broadcast_to(largest, (block, HD))
            total[t, rows, :] = mixed

    def attend_far(g, t):
        key_ext, value_ext = window_of(g, t * tile, far)
        every = [
            lax.dot_general(
                queries(g, t, part), key_ext, (((1,), (1,)), ((), ())),
                preferred_element_type=jnp.float32,
            )
            for part in range(parts)
        ]
        for part, scores in enumerate(every):
            rows = slice(part * block, (part + 1) * block)
            before = peak[t, rows, :]
            largest = jnp.maximum(jnp.max(scores, axis=1, keepdims=True), before)
            fade = jnp.exp2((before - largest) * EXP2_SCALE)
            weights = jnp.exp2(
                (scores - jnp.concatenate([largest] * (far // HD), 1)) * EXP2_SCALE
            )
            mixed = mix(weights, value_ext)
            mixed = total[t, rows, :] * jnp.concatenate([fade, fade], 1) + mixed
            result = (mixed[:, :HD] / mixed[:, HD:]).astype(jnp.bfloat16)
            for m in range(PAIR):
                column = (part * PAIR + m) * HD
                obuf[g, t, :, column:column + HD] = result[m * tile:(m + 1) * tile]

    for g in range(groups):
        def near_step(i, _):
            attend_near(g, (h + n_head - 1 - i) % n_head)
            if g + 1 < groups:
                @pl.when(i == 1)
                def _():
                    relay_one(0, g + 1, 0)
                    relay_one(1, g + 1, 0)
                    relay_two(1, g + 1, 0)

                @pl.when(i == n_head - 1)
                def _():
                    relay_two(0, g + 1, 0)
            return 0

        lax.fori_loop(0, n_head, near_step, 0)
        for a in range(2):
            arrive(g, a)

        def far_step(i, _):
            off = n_head - 1 - i
            t = (h + off) % n_head
            attend_far(g, t)

            @pl.when(i < n_head - 1)
            def _():
                deliver(g, off, t).start()

            @pl.when(i == n_head - 1)
            def _():
                keep(g).start()

            if g + 1 < groups:
                @pl.when(i == n_head // 2)
                def _():
                    relay_one(0, g + 1, 1)
                    relay_one(1, g + 1, 1)
                    relay_two(1, g + 1, 1)

                @pl.when(i == n_head - 1)
                def _():
                    relay_two(0, g + 1, 1)
            return 0

        lax.fori_loop(0, n_head, far_step, 0)

    for g in range(groups):
        for a in range(2):
            sent(g, a)
    for g in range(groups):
        keep(g).wait()
        for off in range(1, n_head):
            deliver(g, off, (h + off) % n_head).wait_send()
            receive(g, off).wait_recv()


def per_device(n_seq, n_head, queries, key_rows, value_rows, doc_lengths):
    tokens = queries.shape[0]
    groups = key_rows.shape[1] // HD
    tile = tokens // n_head
    window = SPAN * tokens
    flops = 4 * tokens * (GROUP * groups) * window * HD
    return pl.pallas_call(
        functools.partial(kernel, n_seq, n_head),
        out_shape=jax.ShapeDtypeStruct((tile, H * HD), jnp.bfloat16),
        in_specs=[pl.BlockSpec(memory_space=pltpu.SMEM)]
        + [pl.BlockSpec(memory_space=pl.ANY)] * 3,
        out_specs=pl.BlockSpec(memory_space=pl.ANY),
        scratch_shapes=[
            pltpu.VMEM((tokens, GROUP * groups * HD), jnp.bfloat16),
            pltpu.VMEM((groups, window, HD), jnp.bfloat16),
            pltpu.VMEM((groups, window, HD), jnp.bfloat16),
            pltpu.VMEM((tokens, HD), jnp.bfloat16),
            pltpu.VMEM((window, HD), jnp.bfloat16),
            pltpu.VMEM((groups, n_head, tile, GROUP * HD), jnp.bfloat16),
            pltpu.VMEM((n_head, GROUP * tile, HD), jnp.float32),
            pltpu.VMEM((n_head, GROUP * tile, 2 * HD), jnp.float32),
            pltpu.SemaphoreType.DMA((groups + 1, 2)),
            pltpu.SemaphoreType.DMA((5, groups, 2)),
            pltpu.SemaphoreType.DMA((SPAN, groups, 2)),
            pltpu.SemaphoreType.DMA((groups, n_head - 1)),
            pltpu.SemaphoreType.DMA((groups, n_head - 1)),
            pltpu.SemaphoreType.DMA((groups,)),
        ],
        compiler_params=pltpu.CompilerParams(
            collective_id=0, has_side_effects=True, vmem_limit_bytes=60 << 20
        ),
        cost_estimate=pl.CostEstimate(flops=flops, bytes_accessed=4 << 20, transcendentals=0),
    )(doc_lengths, queries, key_rows, value_rows)


def solution(mesh):
    body = functools.partial(per_device, mesh.shape["seq"], mesh.shape["head"])
    in_specs = (P("seq", "head"), P("seq", "head"), P("seq", "head"), P())
    out_specs = P(("seq", "head"), None)
    return jax.shard_map(body, mesh=mesh, in_specs=in_specs, out_specs=out_specs, check_vma=False)
```
